32 devices in a mesh: sec: 4 (over y, core), term: 8 (over z, x).
Axes of the slice: x: 2, y: 2, z: 4, core: 2. Of those that a mesh axis runs over, the one named last changes fastest.
Arguments:
- center: float32 [4, 2, 256, 256], P('sec'), may hold values from -6 to 6
- site_maps: float32 [16, 256, 256], P('sec'), may hold values from -1 to 2
- section_sites: int32 [4], P('sec'), may hold values from 1 to 4, 8 in all
- left_edge: float32 [48, 256, 256], P('term'), may hold values from -0.375 to 0.375
- right_edge: float32 [48, 256, 256], P('term'), may hold values from -0.375 to 0.375
- coefficients: float32 [48], replicated, may hold values from -0.875 to 0.875
- term_ids: int32 [48], P('term'), may hold values from 0 to 47, each once
- sector_mask: int32 [48, 2], replicated, may hold values 0 or 1
Outputs:
- evolved: float32 [4, 2, 256, 256], P('sec')
The draws below stay inside these ranges and needn't reach their ends.
Inputs may be any that keep to these rules, and one draw needn't show every extreme that they name: `section_sites`: the sites of all sections sum to 8, and some section has exactly 4. `term_ids`: each of the 48 terms stands in exactly one slot.
All inputs are finite; a program needn't handle non-finite values. No bound on the sum of `section_sites` on one device may be relied on, other than what follows from the above.
Results may differ from the reference program's by a relative error of at most 0.0003.
Values sent between devices are 32-bit elements; how exact they have to be, the bound alone decides.
No kernel may reach another device: no remote copies, remote signals or barrier semaphores. Data moves between devices by JAX's collectives and lax.ppermute only.
A program may use at most 64 MiB of HBM per device.

```python
import math
import jax
import jax.numpy as jnp
import numpy as np
from jax import lax

BOND = 256
SECTORS = 2
SITE_CAP = 4
ORDER = 4
SECTIONS = 4
TERMS = 48
SITES = 16
TOTAL_SITES = 8


def draw_site_maps(key, part):
    noise = jax.random.truncated_normal(key, -4.0, 4.0, (SITES, BOND, BOND), jnp.float32)
    return jnp.eye(BOND, dtype=jnp.float32)[None] + 0.2 / math.sqrt(BOND) * noise


def with_ends(entries, rng, low, top_value):
    extent = entries.shape
    spot = [jax.random.randint(jax.random.fold_in(rng, axis), (), 0, extent[axis]) for axis in range(len(extent))]
    entries = entries.at[tuple(spot)].set(low)
    longest = extent.index(max(extent))
    spot[longest] = (spot[longest] + 1) % extent[longest]
    return entries.at[tuple(spot)].set(top_value)


def block_levels(stream_key, shape, pieces, smallest, largest):
    level = 1.0
    for axis_at, parts in pieces:
        heights = jax.random.uniform(jax.random.fold_in(jax.random.fold_in(stream_key, 6), axis_at), (parts,), jnp.float32, smallest / len(pieces), largest / len(pieces))
        level = level * jnp.repeat(jnp.exp(heights), shape[axis_at] // parts).reshape((-1,) + (1,) * (len(shape) - 1 - axis_at))
    return level


def profile(number_of, total, most, skew):
    weights = [(1 << 20) // math.isqrt(rank ** skew) + 1 for rank in range(2, number_of + 1)]
    rest, holding = total - most - (number_of - 1), [1] * (number_of - 1)
    while rest > 0:
        candidates = [i for i in range(number_of - 1) if holding[i] < most]
        pool, left = sum([weights[i] for i in candidates]), rest
        for i in candidates:
            extra = min(most - holding[i], max(1, left * weights[i] // pool), rest)
            holding[i] = holding[i] + extra
            rest = rest - extra
    return np.array([most] + holding)


def ragged(rng, number_of, total, limit, skew):
    if number_of == 2:
        one = jax.random.randint(rng, (), max(1, total - limit), min(limit, total - 1) + 1)
        return jnp.stack([one, total - one])
    lengths = jnp.asarray(profile(number_of, total, limit, skew), jnp.int32)
    couples = (number_of - 1) // 2
    source_of, sink = lengths[1:1 + 2 * couples:2], lengths[2:2 + 2 * couples:2]
    room = jnp.minimum(source_of - 1, limit - sink)
    shifted = jax.random.randint(jax.random.fold_in(rng, 1), (couples,), 0, 1 << 20) % (room + 1)
    lengths = lengths.at[1:1 + 2 * couples:2].set(source_of - shifted).at[2:2 + 2 * couples:2].set(sink + shifted)
    return lengths[jax.random.permutation(jax.random.fold_in(rng, 2), number_of)]


def centred(stream_key, dims, deviation, limit, pieces=(), held_as=jnp.bfloat16):
    drawn = deviation * jax.random.normal(stream_key, dims, jnp.float32)
    if pieces:
        drawn = drawn * block_levels(stream_key, dims, pieces, -0.22, 0.18)
    return jnp.clip(drawn, -limit, limit).astype(held_as)


def setup_inputs(seed: int = 0) -> dict:
    key_list = jax.random.split(jax.random.key(seed), 9)
    center = centred(key_list[0], (SECTIONS, SECTORS, BOND, BOND), 1.0, 6.0, ((0, 4),), jnp.float32)
    site_maps = draw_site_maps(jax.random.fold_in(key_list[8], 71), 0)
    section_sites = ragged(key_list[2], SECTIONS, TOTAL_SITES, SITE_CAP, 2).astype(jnp.int32)
    left_edge = centred(key_list[3], (TERMS, BOND, BOND), BOND ** -0.5, 0.375, ((0, 8),), jnp.float32)
    right_edge = centred(key_list[4], (TERMS, BOND, BOND), BOND ** -0.5, 0.375, ((0, 8),), jnp.float32)
    coefficients = centred(key_list[5], (TERMS,), TERMS ** -0.5, 0.875, (), jnp.float32)
    term_ids = jax.random.permutation(key_list[6], TERMS).astype(jnp.int32)
    sector_mask = with_ends((jax.random.randint(key_list[7], (TERMS, SECTORS), 0, 3) < 2).astype(jnp.int32), jax.random.fold_in(key_list[7], 1), 0, 1)
    return dict(center=center, site_maps=site_maps, section_sites=section_sites, left_edge=left_edge, right_edge=right_edge, coefficients=coefficients, term_ids=term_ids, sector_mask=sector_mask)


def product(left, right):
    return jnp.dot(left, right, precision=lax.Precision.HIGHEST, preferred_element_type=jnp.float32)


def apply_terms(tensor, env_left, env_right, weight):
    lefted = jnp.einsum("tij,sjk->tsik", env_left, tensor, precision=lax.Precision.HIGHEST)
    lefted = lefted * weight[:, :, None, None]
    return jnp.einsum("tsik,tkl->sil", lefted, env_right, precision=lax.Precision.HIGHEST)


def reference(center, site_maps, section_sites, left_edge, right_edge, coefficients, term_ids, sector_mask):
    width = center.shape[2]
    identity = jnp.eye(width, dtype=jnp.float32)
    slots = site_maps.reshape(SECTIONS, SITE_CAP, width, width)
    section_list = []
    for section in range(SECTIONS):
        running = identity
        for position in range(SITE_CAP):
            running = jnp.where(position < section_sites[section], product(running, slots[section, position]), running)
        section_list.append(running)
    prefixes = [identity]
    for section in range(SECTIONS - 1):
        prefixes.append(product(prefixes[-1], section_list[section]))
    suffixes = [identity]
    for section in range(SECTIONS - 1, 0, -1):
        suffixes.append(product(section_list[section], suffixes[-1]))
    suffixes = suffixes[::-1]
    weight = coefficients[term_ids][:, None] * sector_mask[term_ids].astype(jnp.float32)
    results = []
    for section in range(SECTIONS):
        prefix = prefixes[section]
        suffix = suffixes[section]
        lefted = jnp.einsum("tjk,kl->tjl", left_edge, prefix, precision=lax.Precision.HIGHEST)
        env_left = jnp.einsum("ji,tjl->til", prefix, lefted, precision=lax.Precision.HIGHEST)
        righted = jnp.einsum("ij,tjk->tik", suffix, right_edge, precision=lax.Precision.HIGHEST)
        env_right = jnp.einsum("tik,lk->til", righted, suffix, precision=lax.Precision.HIGHEST)
        current = center[section]
        evolved = current
        for order in range(1, ORDER + 1):
            current = apply_terms(current, env_left, env_right, weight) * (-0.3 / order)
            evolved = evolved + current
        results.append(evolved)
    return jnp.stack(results)
```

```python
import functools

import jax
import jax.numpy as jnp
from jax import lax
from jax.sharding import PartitionSpec as P

ORDER = 4
TAYLOR_STEP = 0.3
PAIR = 2


def product(left, right):
    return jnp.dot(left, right, precision=lax.Precision.HIGH, preferred_element_type=jnp.float32)


def swap(value, axis, bit):
    pairs = [(i, i ^ bit) for i in range(lax.axis_size(axis))]
    return lax.ppermute(value, axis, pairs)


def section_product(slots, count):
    factors = [slots[i] for i in range(slots.shape[0])]
    starts = list(range(len(factors)))
    while len(factors) > 1:
        merged, merged_starts = [], []
        for i in range(0, len(factors), 2):
            if i + 1 == len(factors):
                merged.append(factors[i])
            else:
                both = product(factors[i], factors[i + 1])
                merged.append(jnp.where(starts[i + 1] < count, both, factors[i]))
            merged_starts.append(starts[i])
        factors, starts = merged, merged_starts
    return factors[0]


def scan_maps(section_map):
    position = lax.axis_index("sec")
    sections = lax.axis_size("sec")
    segment = section_map
    identity = jnp.eye(section_map.shape[0], dtype=jnp.float32)
    prefix = suffix = identity
    bit = 1
    while bit < sections:
        other = swap(segment, "sec", bit)
        upper = (position & bit) != 0
        if bit == 1:
            prefix = jnp.where(upper, other, identity)
            suffix = jnp.where(upper, identity, other)
        else:
            grown = product(jnp.where(upper, other, suffix), jnp.where(upper, prefix, other))
            prefix = jnp.where(upper, grown, prefix)
            suffix = jnp.where(upper, suffix, grown)
        if 2 * bit < sections:
            segment = product(
                jnp.where(upper, other, segment), jnp.where(upper, segment, other)
            )
        bit *= 2
    return prefix, suffix


def reduce_chunks(partial, group, groups):
    chunks = partial.reshape(groups, partial.shape[0] // groups, partial.shape[1])
    pick = functools.partial(lax.dynamic_index_in_dim, chunks, axis=0, keepdims=False)
    arrived = [swap(pick(group ^ d), "term", PAIR * d) for d in range(1, groups)]
    return sum(arrived, pick(group))


def gather_chunks(chunk, group, groups):
    arrived = [swap(chunk, "term", PAIR * d) for d in range(1, groups)]
    whole = jnp.zeros((groups,) + chunk.shape, chunk.dtype)
    whole = lax.dynamic_update_index_in_dim(whole, chunk, group, 0)
    for d in range(1, groups):
        whole = lax.dynamic_update_index_in_dim(whole, arrived[d - 1], group ^ d, 0)
    return whole.reshape(groups * chunk.shape[0], chunk.shape[1])


def apply_terms(tensor, lefts, rights):
    terms, width = lefts.shape[0], tensor.shape[0]
    lefted = product(lefts.reshape(terms * width, width), tensor).reshape(terms, width, width)
    return jnp.einsum(
        "tik,tkl->il", lefted, rights, precision=lax.Precision.HIGH,
        preferred_element_type=jnp.float32,
    )


def on_device(
    center, site_maps, section_sites, left_edge, right_edge, coefficients, term_ids, sector_mask
):
    width = center.shape[2]
    slots = left_edge.shape[0]
    half = slots // 2
    groups = lax.axis_size("term") // PAIR
    place = lax.axis_index("term")
    group, mine = place // PAIR, place % PAIR
    spot = lax.axis_index("sec")
    core, side = spot & 1, (spot >> 1) & 1

    chosen = term_ids[:, None] == jnp.arange(coefficients.shape[0], dtype=jnp.int32)[None, :]
    slot_weight = jnp.sum(jnp.where(chosen, coefficients[None, :], 0.0), axis=1)
    slot_mask = jnp.sum(
        jnp.where(chosen[:, :, None], sector_mask.astype(jnp.float32)[None], 0.0), axis=1
    )
    weight = slot_weight[:, None] * slot_mask

    for_other = jnp.where(mine == 0, weight[:, 1], weight[:, 0])
    for_mine = jnp.where(mine == 0, weight[:, 0], weight[:, 1])
    quarter = jnp.where(
        core == 0,
        lax.dynamic_slice_in_dim(left_edge, side * half, half, 0)
        * lax.dynamic_slice_in_dim(for_other, side * half, half, 0)[:, None, None],
        lax.dynamic_slice_in_dim(right_edge, side * half, half, 0),
    )
    quarter = swap(quarter, "term", 1)
    halves = jnp.concatenate([quarter, swap(quarter, "sec", 2)], axis=0)
    traded = swap(halves, "sec", 1)
    other_left = jnp.where(core == 0, halves, traded)
    other_right = jnp.where(core == 0, traded, halves)

    section_map = section_product(site_maps, section_sites[0])
    prefix, suffix = scan_maps(section_map)

    base = center[0]
    turned = product(jnp.einsum("ij,sjk->sik", prefix, base, precision=lax.Precision.HIGH)
                     .reshape(PAIR * width, width), suffix).reshape(PAIR, width, width)

    lefted = jnp.einsum("tij,sjk->tsik", left_edge, turned, precision=lax.Precision.HIGH)
    lefted = lefted * weight[:, :, None, None]
    partial = jnp.einsum("tsik,tkl->sil", lefted, right_edge, precision=lax.Precision.HIGH)
    keep = lax.dynamic_index_in_dim(partial, mine, 0, keepdims=False)
    give = lax.dynamic_index_in_dim(partial, 1 - mine, 0, keepdims=False)
    partial = keep + swap(give, "term", 1)
    current = gather_chunks(
        reduce_chunks(partial, group, groups) * (-TAYLOR_STEP), group, groups
    )
    total = current

    gram_left = jnp.einsum("ij,kj->ik", prefix, prefix, precision=lax.Precision.HIGH)
    gram_right = jnp.einsum("ji,jk->ik", suffix, suffix, precision=lax.Precision.HIGH)
    lefts = jnp.concatenate([left_edge * for_mine[:, None, None], other_left], axis=0)
    rights = jnp.concatenate([right_edge, other_right], axis=0)
    lefts = product(lefts.reshape(-1, width), gram_left).reshape(lefts.shape)
    rights = jnp.einsum("ij,tjk->tik", gram_right, rights, precision=lax.Precision.HIGH)
    lefts_out = jnp.einsum("ji,tjk->tik", prefix, lefts, precision=lax.Precision.HIGH)
    rights_out = jnp.einsum("tij,kj->tik", rights, suffix, precision=lax.Precision.HIGH)

    for order in range(2, ORDER):
        partial = apply_terms(current, lefts, rights)
        current = gather_chunks(
            reduce_chunks(partial, group, groups) * (-TAYLOR_STEP / order), group, groups
        )
        total = total + current

    partial = apply_terms(current, lefts_out, rights_out)
    start = lax.dynamic_index_in_dim(base, mine, 0, keepdims=False)
    back = product(jnp.einsum("ji,jk->ik", prefix, total, precision=lax.Precision.HIGH), suffix.T)
    so_far = (start + back).reshape(groups, width // groups, width)
    chunk = reduce_chunks(partial, group, groups) * (-TAYLOR_STEP / ORDER)
    chunk = chunk + lax.dynamic_index_in_dim(so_far, group, 0, keepdims=False)
    other_chunk = swap(chunk, "term", 1)
    ours = gather_chunks(chunk, group, groups)
    theirs = gather_chunks(other_chunk, group, groups)
    evolved = jnp.stack(
        [jnp.where(mine == 0, ours, theirs), jnp.where(mine == 0, theirs, ours)]
    )
    return evolved[None]


def solution(mesh):
    in_specs = (
        P("sec", None, None, None),
        P("sec", None, None),
        P("sec"),
        P("term", None, None),
        P("term", None, None),
        P(),
        P("term"),
        P(),
    )
    out_specs = P("sec", None, None, None)
    return jax.shard_map(
        on_device, mesh=mesh, in_specs=in_specs, out_specs=out_specs, check_vma=False
    )
```

```python
import functools

import jax
import jax.numpy as jnp
from jax import lax
from jax.sharding import PartitionSpec as P


ORDER = 4
TAYLOR_STEP = 0.3
PAIR = 2


def product(left, right):
    return jnp.dot(left, right, precision=lax.Precision.HIGH, preferred_element_type=jnp.float32)


def swap(value, axis, bit):
    pairs = [(i, i ^ bit) for i in range(lax.axis_size(axis))]
    return lax.ppermute(value, axis, pairs)


def section_product(slots, count):
    factors = [slots[i] for i in range(slots.shape[0])]
    starts = list(range(len(factors)))
    while len(factors) > 1:
        merged, merged_starts = [], []
        for i in range(0, len(factors), 2):
            if i + 1 == len(factors):
                merged.append(factors[i])
            else:
                both = product(factors[i], factors[i + 1])
                merged.append(jnp.where(starts[i + 1] < count, both, factors[i]))
            merged_starts.append(starts[i])
        factors, starts = merged, merged_starts
    return factors[0]


def scan_maps(section_map):
    position = lax.axis_index("sec")
    sections = lax.axis_size("sec")
    segment = section_map
    identity = jnp.eye(section_map.shape[0], dtype=jnp.float32)
    prefix = suffix = identity
    bit = 1
    while bit < sections:
        other = swap(segment, "sec", bit)
        upper = (position & bit) != 0
        if bit == 1:
            prefix = jnp.where(upper, other, identity)
            suffix = jnp.where(upper, identity, other)
        else:
            grown = product(jnp.where(upper, other, suffix), jnp.where(upper, prefix, other))
            prefix = jnp.where(upper, grown, prefix)
            suffix = jnp.where(upper, suffix, grown)
        if 2 * bit < sections:
            segment = product(
                jnp.where(upper, other, segment), jnp.where(upper, segment, other)
            )
        bit *= 2
    return prefix, suffix


def reduce_chunks(partial, group, groups):
    chunks = partial.reshape(groups, partial.shape[0] // groups, partial.shape[1])
    pick = functools.partial(lax.dynamic_index_in_dim, chunks, axis=0, keepdims=False)
    arrived = [swap(pick(group ^ d), "term", PAIR * d) for d in range(1, groups)]
    return sum(arrived, pick(group))


def gather_chunks(chunk, group, groups):
    arrived = [swap(chunk, "term", PAIR * d) for d in range(1, groups)]
    whole = jnp.zeros((groups,) + chunk.shape, chunk.dtype)
    whole = lax.dynamic_update_index_in_dim(whole, chunk, group, 0)
    for d in range(1, groups):
        whole = lax.dynamic_update_index_in_dim(whole, arrived[d - 1], group ^ d, 0)
    return whole.reshape(groups * chunk.shape[0], chunk.shape[1])


def apply_terms(tensor, lefts, rights):
    terms, width = lefts.shape[0], tensor.shape[0]
    lefted = product(lefts.reshape(terms * width, width), tensor).reshape(terms, width, width)
    return jnp.einsum(
        "tik,tkl->il", lefted, rights, precision=lax.Precision.HIGH,
        preferred_element_type=jnp.float32,
    )


def on_device(
    center, site_maps, section_sites, left_edge, right_edge, coefficients, term_ids, sector_mask
):
    width = center.shape[2]
    slots = left_edge.shape[0]
    half = slots // 2
    groups = lax.axis_size("term") // PAIR
    place = lax.axis_index("term")
    group, mine = place // PAIR, place % PAIR
    spot = lax.axis_index("sec")
    core, side = spot & 1, (spot >> 1) & 1

    chosen = term_ids[:, None] == jnp.arange(coefficients.shape[0], dtype=jnp.int32)[None, :]
    slot_weight = jnp.sum(jnp.where(chosen, coefficients[None, :], 0.0), axis=1)
    slot_mask = jnp.sum(
        jnp.where(chosen[:, :, None], sector_mask.astype(jnp.float32)[None], 0.0), axis=1
    )
    weight = slot_weight[:, None] * slot_mask

    quarter = jnp.where(
        core == 0,
        lax.dynamic_slice_in_dim(left_edge, side * half, half, 0),
        lax.dynamic_slice_in_dim(right_edge, side * half, half, 0),
    ).reshape(2, half * width // 2, width)
    pieces = [swap(quarter[i], "term", 1) for i in range(2)]
    shared = [swap(pieces[i], "sec", 2) for i in range(2)]
    halves = jnp.concatenate(pieces + shared, axis=0).reshape(slots, width, width)
    traded = swap(halves, "sec", 1)
    for_mine = jnp.where(mine == 0, weight[:, 0], weight[:, 1])
    others = swap(jnp.where(mine == 0, weight[:, 1], weight[:, 0]), "term", 1)
    others = jnp.where(side == 0, others, jnp.roll(others, half))
    other_left = jnp.where(core == 0, halves, traded) * others[:, None, None]
    other_right = jnp.where(core == 0, traded, halves)

    section_map = section_product(site_maps, section_sites[0])
    prefix, suffix = scan_maps(section_map)

    base = center[0]
    turned = product(jnp.einsum("ij,sjk->sik", prefix, base, precision=lax.Precision.HIGH)
                     .reshape(PAIR * width, width), suffix).reshape(PAIR, width, width)

    lefted = jnp.einsum("tij,sjk->tsik", left_edge, turned, precision=lax.Precision.HIGH)
    lefted = lefted * weight[:, :, None, None]
    partial = jnp.einsum("tsik,tkl->sil", lefted, right_edge, precision=lax.Precision.HIGH)
    keep = lax.dynamic_index_in_dim(partial, mine, 0, keepdims=False)
    give = lax.dynamic_index_in_dim(partial, 1 - mine, 0, keepdims=False)
    partial = keep + swap(give, "term", 1)
    current = gather_chunks(reduce_chunks(partial, group, groups) * (-TAYLOR_STEP), group, groups)
    total = current

    gram_left = jnp.einsum("ij,kj->ik", prefix, prefix, precision=lax.Precision.HIGH)
    gram_right = jnp.einsum("ji,jk->ik", suffix, suffix, precision=lax.Precision.HIGH)
    lefts = jnp.concatenate([left_edge * for_mine[:, None, None], other_left], axis=0)
    rights = jnp.concatenate([right_edge, other_right], axis=0)
    lefts = product(lefts.reshape(-1, width), gram_left).reshape(lefts.shape)
    rights = jnp.einsum("ij,tjk->tik", gram_right, rights, precision=lax.Precision.HIGH)
    lefts_out = jnp.einsum("ji,tjk->tik", prefix, lefts, precision=lax.Precision.HIGH)
    rights_out = jnp.einsum("tij,kj->tik", rights, suffix, precision=lax.Precision.HIGH)

    for order in range(2, ORDER):
        partial = apply_terms(current, lefts, rights)
        current = reduce_chunks(partial, group, groups) * (-TAYLOR_STEP / order)
        current = gather_chunks(current, group, groups)
        total = total + current

    partial = apply_terms(current, lefts_out, rights_out)
    start = lax.dynamic_index_in_dim(base, mine, 0, keepdims=False)
    back = product(jnp.einsum("ji,jk->ik", prefix, total, precision=lax.Precision.HIGH), suffix.T)
    so_far = (start + back).reshape(groups, width // groups, width)
    chunk = reduce_chunks(partial, group, groups) * (-TAYLOR_STEP / ORDER)
    chunk = chunk + lax.dynamic_index_in_dim(so_far, group, 0, keepdims=False)
    other_chunk = swap(chunk, "term", 1)
    ours = gather_chunks(chunk, group, groups)
    theirs = gather_chunks(other_chunk, group, groups)
    evolved = jnp.stack(
        [jnp.where(mine == 0, ours, theirs), jnp.where(mine == 0, theirs, ours)]
    )
    return evolved[None]


def solution(mesh):
    in_specs = (
        P("sec", None, None, None),
        P("sec", None, None),
        P("sec"),
        P("term", None, None),
        P("term", None, None),
        P(),
        P("term"),
        P(),
    )
    out_specs = P("sec", None, None, None)
    return jax.shard_map(
        on_device, mesh=mesh, in_specs=in_specs, out_specs=out_specs, check_vma=False
    )
```

```python
import jax
import jax.numpy as jnp
from jax import lax
from jax.sharding import PartitionSpec as P

ORDER = 4
TAYLOR_STEP = 0.3
PAIR = 2


def product(left, right):
    return jnp.dot(left, right, precision=lax.Precision.HIGH, preferred_element_type=jnp.float32)


def contract(spec, left, right):
    return jnp.einsum(
        spec, left, right, precision=lax.Precision.HIGH, preferred_element_type=jnp.float32
    )


def swap(value, axis, mask):
    pairs = [(i, i ^ mask) for i in range(lax.axis_size(axis))]
    return lax.ppermute(value, axis, pairs)


def sum_masks():
    size = lax.axis_size("term")
    masks = [1]
    if size >= 8:
        masks.append(6)
    bit = 8
    while bit < size:
        masks.append(bit)
        bit *= 2
    return masks


def section_product(slots, count):
    factors = [slots[i] for i in range(slots.shape[0])]
    starts = list(range(len(factors)))
    while len(factors) > 1:
        merged, merged_starts = [], []
        for i in range(0, len(factors), 2):
            if i + 1 == len(factors):
                merged.append(factors[i])
            else:
                both = product(factors[i], factors[i + 1])
                merged.append(jnp.where(starts[i + 1] < count, both, factors[i]))
            merged_starts.append(starts[i])
        factors, starts = merged, merged_starts
    return factors[0]


def scan_maps(section_map):
    position = lax.axis_index("sec")
    sections = lax.axis_size("sec")
    segment = section_map
    identity = jnp.eye(section_map.shape[0], dtype=jnp.float32)
    prefix = suffix = identity
    bit = 1
    while bit < sections:
        other = swap(segment, "sec", bit)
        upper = (position & bit) != 0
        if bit == 1:
            prefix = jnp.where(upper, other, identity)
            suffix = jnp.where(upper, identity, other)
        else:
            grown = product(jnp.where(upper, other, suffix), jnp.where(upper, prefix, other))
            prefix = jnp.where(upper, grown, prefix)
            suffix = jnp.where(upper, suffix, grown)
        if 2 * bit < sections:
            segment = product(
                jnp.where(upper, other, segment), jnp.where(upper, segment, other)
            )
        bit *= 2
    return prefix, suffix


def sum_groups(partial):
    masks = sum_masks()
    half = partial.shape[0] // 2
    upper, lower = partial[:half], partial[half:]
    for i in range(len(masks)):
        upper, lower = (
            upper + swap(upper, "term", masks[i]), lower + swap(lower, "term", masks[-1 - i])
        )
    return upper, lower


def apply_terms(tensor, lefts, rights):
    return contract("tik,tkl->il", contract("tij,jk->tik", lefts, tensor), rights)


def on_device(
    center, site_maps, section_sites, left_edge, right_edge, coefficients, term_ids, sector_mask
):
    width = center.shape[2]
    slots = left_edge.shape[0]
    half = slots // 2
    piece = half * width // 2
    place = lax.axis_index("term")
    mine = ((place >> 1) ^ (place >> 2)) & 1
    spot = lax.axis_index("sec")
    core, side = spot & 1, (spot >> 1) & 1

    chosen = term_ids[:, None] == jnp.arange(coefficients.shape[0], dtype=jnp.int32)[None, :]
    slot_weight = jnp.sum(jnp.where(chosen, coefficients[None, :], 0.0), axis=1)
    slot_mask = jnp.sum(
        jnp.where(chosen[:, :, None], sector_mask.astype(jnp.float32)[None], 0.0), axis=1
    )
    weight = slot_weight[:, None] * slot_mask
    keep_weight = jnp.where(mine == 0, weight[:, 0], weight[:, 1])
    give_weight = jnp.where(mine == 0, weight[:, 1], weight[:, 0])

    flat_left = left_edge.reshape(slots * width, width)
    flat_right = right_edge.reshape(slots * width, width)
    pieces = []
    for i in range(2):
        start = side * (half * width) + i * piece
        cut = jnp.where(
            core == 0,
            lax.dynamic_slice_in_dim(flat_left, start, piece, 0),
            lax.dynamic_slice_in_dim(flat_right, start, piece, 0),
        )
        pieces.append(swap(cut, "term", PAIR))
    shared = [swap(pieces[i], "sec", 2) for i in range(2)]
    halves = jnp.concatenate(pieces + shared, axis=0).reshape(slots, width, width)
    traded = swap(halves, "sec", 1)
    others = swap(give_weight, "term", PAIR)
    others = jnp.where(side == 0, others, jnp.roll(others, half))
    other_left = jnp.where(core == 0, halves, traded) * others[:, None, None]
    other_right = jnp.where(core == 0, traded, halves)

    section_map = section_product(site_maps, section_sites[0])
    prefix, suffix = scan_maps(section_map)

    base = center[0]
    start_keep = lax.dynamic_index_in_dim(base, mine, 0, keepdims=False)
    start_give = lax.dynamic_index_in_dim(base, 1 - mine, 0, keepdims=False)

    def first(start, weights):
        turned = product(product(prefix, start), suffix)
        lefted = contract("tij,jk->tik", left_edge, turned) * weights[:, None, None]
        return contract("tik,tkl->il", lefted, right_edge)

    given = first(start_give, give_weight)
    kept = first(start_keep, keep_weight)
    partial = kept + swap(given, "term", PAIR)
    current = jnp.concatenate(sum_groups(partial), axis=0) * (-TAYLOR_STEP)
    total = current

    gram_left = contract("ij,kj->ik", prefix, prefix)
    gram_right = contract("ji,jk->ik", suffix, suffix)
    own_left = left_edge * keep_weight[:, None, None]

    turned = product(product(gram_left, current), gram_right)
    partial = apply_terms(turned, own_left, right_edge)
    partial = partial + apply_terms(turned, other_left, other_right)
    current = jnp.concatenate(sum_groups(partial), axis=0) * (-TAYLOR_STEP / 2)
    total = total + current

    lefts = jnp.concatenate([own_left, other_left], axis=0)
    rights = jnp.concatenate([right_edge, other_right], axis=0)
    lefts = contract("tij,jk->tik", lefts, gram_left)
    rights = contract("ij,tjk->tik", gram_right, rights)
    lefts_out = contract("ji,tjk->tik", prefix, lefts)
    rights_out = contract("tij,kj->tik", rights, suffix)

    for order in range(3, ORDER):
        partial = apply_terms(current, lefts, rights)
        current = jnp.concatenate(sum_groups(partial), axis=0)
        current = current * (-TAYLOR_STEP / order)
        total = total + current

    partial = apply_terms(current, lefts_out, rights_out) * (-TAYLOR_STEP / ORDER)
    so_far = start_keep + contract("ij,kj->ik", contract("ji,jk->ik", prefix, total), suffix)
    ends = sum_groups(partial)
    ours, theirs = [], []
    for i, end in enumerate(ends):
        rows = end.shape[0]
        end = so_far[i * rows : (i + 1) * rows] + end
        ours.append(end)
        theirs.append(swap(end, "term", PAIR))
    ours, theirs = jnp.concatenate(ours, axis=0), jnp.concatenate(theirs, axis=0)
    evolved = jnp.stack(
        [jnp.where(mine == 0, ours, theirs), jnp.where(mine == 0, theirs, ours)]
    )
    return evolved[None]


def solution(mesh):
    in_specs = (
        P("sec", None, None, None),
        P("sec", None, None),
        P("sec"),
        P("term", None, None),
        P("term", None, None),
        P(),
        P("term"),
        P(),
    )
    out_specs = P("sec", None, None, None)
    return jax.shard_map(
        on_device, mesh=mesh, in_specs=in_specs, out_specs=out_specs, check_vma=False
    )
```

```python
import jax
import jax.numpy as jnp
from jax import lax
from jax.sharding import PartitionSpec as P

ORDER = 4
TAYLOR_STEP = 0.3
PAIR = 2


def product(left, right):
    return jnp.dot(left, right, precision=lax.Precision.HIGH, preferred_element_type=jnp.float32)


def contract(spec, left, right):
    return jnp.einsum(
        spec, left, right, precision=lax.Precision.HIGH, preferred_element_type=jnp.float32
    )


def swap(value, axis, mask):
    pairs = [(i, i ^ mask) for i in range(lax.axis_size(axis))]
    return lax.ppermute(value, axis, pairs)


def sum_masks():
    size = lax.axis_size("term")
    masks = [1]
    if size >= 8:
        masks.append(6)
    bit = 8
    while bit < size:
        masks.append(bit)
        bit *= 2
    return masks


def section_product(slots, count):
    factors = [slots[i] for i in range(slots.shape[0])]
    starts = list(range(len(factors)))
    while len(factors) > 1:
        merged, merged_starts = [], []
        for i in range(0, len(factors), 2):
            if i + 1 == len(factors):
                merged.append(factors[i])
            else:
                both = product(factors[i], factors[i + 1])
                merged.append(jnp.where(starts[i + 1] < count, both, factors[i]))
            merged_starts.append(starts[i])
        factors, starts = merged, merged_starts
    return factors[0]


def scan_maps(section_map):
    position = lax.axis_index("sec")
    sections = lax.axis_size("sec")
    segment = section_map
    identity = jnp.eye(section_map.shape[0], dtype=jnp.float32)
    prefix = suffix = identity
    bit = 1
    while bit < sections:
        other = swap(segment, "sec", bit)
        upper = (position & bit) != 0
        if bit == 1:
            prefix = jnp.where(upper, other, identity)
            suffix = jnp.where(upper, identity, other)
        else:
            grown = product(jnp.where(upper, other, suffix), jnp.where(upper, prefix, other))
            prefix = jnp.where(upper, grown, prefix)
            suffix = jnp.where(upper, suffix, grown)
        if 2 * bit < sections:
            segment = product(
                jnp.where(upper, other, segment), jnp.where(upper, segment, other)
            )
        bit *= 2
    return prefix, suffix


def sum_groups(partial):
    masks = sum_masks()
    half = partial.shape[0] // 2
    upper = lax.optimization_barrier(partial[:half])
    lower = lax.optimization_barrier(partial[half:])
    for i in range(len(masks)):
        from_upper = swap(upper, "term", masks[i])
        from_lower = swap(lower, "term", masks[-1 - i])
        upper, lower = upper + from_upper, lower + from_lower
    return upper, lower


def apply_terms(tensor, lefts, rights, weights=None):
    lefted = contract("tij,jk->tik", lefts, tensor)
    if weights is not None:
        lefted = lax.optimization_barrier(lefted * weights[:, None, None])
    return contract("tik,tkl->il", lefted, rights)


def on_device(
    center, site_maps, section_sites, left_edge, right_edge, coefficients, term_ids, sector_mask
):
    width = center.shape[2]
    slots = left_edge.shape[0]
    half = slots // 2
    place = lax.axis_index("term")
    mine = ((place >> 1) ^ (place >> 2)) & 1
    spot = lax.axis_index("sec")
    core, side = spot & 1, (spot >> 1) & 1

    chosen = term_ids[:, None] == jnp.arange(coefficients.shape[0], dtype=jnp.int32)[None, :]
    slot_weight = jnp.sum(jnp.where(chosen, coefficients[None, :], 0.0), axis=1)
    slot_mask = jnp.sum(
        jnp.where(chosen[:, :, None], sector_mask.astype(jnp.float32)[None], 0.0), axis=1
    )
    weight = slot_weight[:, None] * slot_mask
    keep_weight = jnp.where(mine == 0, weight[:, 0], weight[:, 1])
    give_weight = jnp.where(mine == 0, weight[:, 1], weight[:, 0])

    rows = slots * width // 4
    place_in_four = (2 * side + core) * rows
    ends = []
    cuts = [
        lax.dynamic_slice_in_dim(edge.reshape(-1, width), place_in_four, rows, 0)
        for edge in (left_edge, right_edge)
    ]
    site_maps, *cuts = lax.optimization_barrier([site_maps] + cuts)
    for cut in cuts:
        near = swap(cut, "term", PAIR)
        far = swap(near, "sec", 2)
        held = jnp.stack([near, far])
        traded = swap(held, "sec", 1)
        held, traded = jnp.where(core == 0, held, traded), jnp.where(core == 0, traded, held)
        ends.append(jnp.stack([held, traded], axis=1).reshape(slots, width, width))
    other_left, other_right = ends
    others = swap(give_weight, "term", PAIR)
    others = jnp.where(side == 0, others, jnp.roll(others, half))

    section_map = section_product(site_maps, section_sites[0])
    prefix, suffix = scan_maps(section_map)

    base = center[0]
    start_keep = lax.dynamic_index_in_dim(base, mine, 0, keepdims=False)
    start_give = lax.dynamic_index_in_dim(base, 1 - mine, 0, keepdims=False)

    def first(start, weights):
        turned = product(product(prefix, start), suffix)
        return apply_terms(turned, left_edge, right_edge, weights)

    given = first(start_give, give_weight)
    kept = first(start_keep, keep_weight)
    partial = kept + swap(given, "term", PAIR)
    current = jnp.concatenate(sum_groups(partial), axis=0) * (-TAYLOR_STEP)
    total = current

    gram_left = contract("ij,kj->ik", prefix, prefix)
    gram_right = contract("ji,jk->ik", suffix, suffix)

    turned = product(product(gram_left, current), gram_right)
    partial = apply_terms(turned, left_edge, right_edge, keep_weight)
    partial = partial + apply_terms(turned, other_left, other_right, others)
    current = jnp.concatenate(sum_groups(partial), axis=0) * (-TAYLOR_STEP / 2)
    total = total + current

    weights = jnp.concatenate([keep_weight, others])
    lefts = jnp.concatenate([left_edge, other_left], axis=0)
    rights = jnp.concatenate([right_edge, other_right], axis=0)
    lefts = contract("tij,jk->tik", lefts, gram_left) * weights[:, None, None]
    rights = contract("ij,tjk->tik", gram_right, rights)

    for order in range(3, ORDER):
        partial = apply_terms(current, lefts, rights)
        current = jnp.concatenate(sum_groups(partial), axis=0)
        current = current * (-TAYLOR_STEP / order)
        total = total + current

    partial = apply_terms(current, lefts, rights) * (-TAYLOR_STEP / ORDER)
    partial = contract("ij,kj->ik", contract("ji,jk->ik", prefix, partial), suffix)
    so_far = start_keep + contract("ij,kj->ik", contract("ji,jk->ik", prefix, total), suffix)
    ends = sum_groups(partial)
    ours, theirs = [], []
    for i, end in enumerate(ends):
        rows = end.shape[0]
        end = so_far[i * rows : (i + 1) * rows] + end
        ours.append(end)
        theirs.append(swap(end, "term", PAIR))
    ours, theirs = jnp.concatenate(ours, axis=0), jnp.concatenate(theirs, axis=0)
    evolved = jnp.stack(
        [jnp.where(mine == 0, ours, theirs), jnp.where(mine == 0, theirs, ours)]
    )
    return evolved[None]


def solution(mesh):
    in_specs = (
        P("sec", None, None, None),
        P("sec", None, None),
        P("sec"),
        P("term", None, None),
        P("term", None, None),
        P(),
        P("term"),
        P(),
    )
    out_specs = P("sec", None, None, None)
    return jax.shard_map(
        on_device, mesh=mesh, in_specs=in_specs, out_specs=out_specs, check_vma=False
    )
```

```python
import jax
import jax.numpy as jnp
from jax import lax
from jax.experimental.layout import Layout, with_layout_constraint
from jax.sharding import PartitionSpec as P

ORDER = 4
TAYLOR_STEP = 0.3
PAIR = 2


def product(left, right):
    return jnp.dot(left, right, precision=lax.Precision.HIGH, preferred_element_type=jnp.float32)


def contract(spec, left, right):
    return jnp.einsum(
        spec, left, right, precision=lax.Precision.HIGH, preferred_element_type=jnp.float32
    )


def swap(value, axis, mask):
    pairs = [(i, i ^ mask) for i in range(lax.axis_size(axis))]
    return lax.ppermute(value, axis, pairs)


def sum_masks():
    size = lax.axis_size("term")
    masks = [1]
    if size >= 8:
        masks.append(6)
    bit = 8
    while bit < size:
        masks.append(bit)
        bit *= 2
    return masks


def section_product(slots, count):
    factors = [slots[i] for i in range(slots.shape[0])]
    starts = list(range(len(factors)))
    while len(factors) > 1:
        merged, merged_starts = [], []
        for i in range(0, len(factors), 2):
            if i + 1 == len(factors):
                merged.append(factors[i])
            else:
                both = product(factors[i], factors[i + 1])
                merged.append(jnp.where(starts[i + 1] < count, both, factors[i]))
            merged_starts.append(starts[i])
        factors, starts = merged, merged_starts
    return factors[0]


def scan_maps(section_map):
    position = lax.axis_index("sec")
    sections = lax.axis_size("sec")
    segment = section_map
    identity = jnp.eye(section_map.shape[0], dtype=jnp.float32)
    prefix = suffix = identity
    bit = 1
    while bit < sections:
        other = swap(segment, "sec", bit)
        upper = (position & bit) != 0
        if bit == 1:
            prefix = jnp.where(upper, other, identity)
            suffix = jnp.where(upper, identity, other)
        else:
            grown = product(jnp.where(upper, other, suffix), jnp.where(upper, prefix, other))
            prefix = jnp.where(upper, grown, prefix)
            suffix = jnp.where(upper, suffix, grown)
        if 2 * bit < sections:
            segment = product(
                jnp.where(upper, other, segment), jnp.where(upper, segment, other)
            )
        bit *= 2
    return prefix, suffix


def sum_groups(partial):
    masks = sum_masks()
    half = partial.shape[0] // 2
    upper = lax.optimization_barrier(partial[:half])
    lower = lax.optimization_barrier(partial[half:])
    for i in range(len(masks)):
        from_upper = swap(upper, "term", masks[i])
        from_lower = swap(lower, "term", masks[-1 - i])
        upper = upper + from_upper
        lower = lower + from_lower
    return upper, lower


def apply_terms(tensor, lefts, rights, weights=None):
    lefted = contract("tij,jk->tik", lefts, tensor)
    if weights is not None:
        lefted = lax.optimization_barrier(lefted * weights[:, None, None])
    lefted = with_layout_constraint(lefted, Layout(major_to_minor=(0, 1, 2)))
    return contract("tik,tkl->il", lefted, rights)


def on_device(
    center, site_maps, section_sites, left_edge, right_edge, coefficients, term_ids, sector_mask
):
    width = center.shape[2]
    slots = left_edge.shape[0]
    half = slots // 2
    place = lax.axis_index("term")
    mine = ((place >> 1) ^ (place >> 2)) & 1
    spot = lax.axis_index("sec")
    core, side = spot & 1, (spot >> 1) & 1

    chosen = term_ids[:, None] == jnp.arange(coefficients.shape[0], dtype=jnp.int32)[None, :]
    slot_weight = jnp.sum(jnp.where(chosen, coefficients[None, :], 0.0), axis=1)
    slot_mask = jnp.sum(
        jnp.where(chosen[:, :, None], sector_mask.astype(jnp.float32)[None], 0.0), axis=1
    )
    weight = slot_weight[:, None] * slot_mask
    keep_weight = jnp.where(mine == 0, weight[:, 0], weight[:, 1])
    give_weight = jnp.where(mine == 0, weight[:, 1], weight[:, 0])

    rows = slots * width // 4
    place_in_four = (2 * side + core) * rows
    ends = []
    cuts = [
        lax.dynamic_slice_in_dim(edge.reshape(-1, width), place_in_four, rows, 0)
        for edge in (left_edge, right_edge)
    ]
    site_maps, *cuts = lax.optimization_barrier([site_maps] + cuts)
    for cut in cuts:
        near = swap(cut, "term", PAIR)
        far = swap(near, "sec", 2)
        held = jnp.stack([near, far])
        traded = swap(held, "sec", 1)
        held, traded = jnp.where(core == 0, held, traded), jnp.where(core == 0, traded, held)
        ends.append(jnp.stack([held, traded], axis=1).reshape(slots, width, width))
    other_left, other_right = ends
    others = swap(give_weight, "term", PAIR)
    others = jnp.where(side == 0, others, jnp.roll(others, half))

    section_map = section_product(site_maps, section_sites[0])
    prefix, suffix = scan_maps(section_map)

    base = center[0]
    start_keep = lax.dynamic_index_in_dim(base, mine, 0, keepdims=False)
    start_give = lax.dynamic_index_in_dim(base, 1 - mine, 0, keepdims=False)

    def first(start, weights):
        turned = product(product(prefix, start), suffix)
        return apply_terms(turned, left_edge, right_edge, weights)

    given = first(start_give, give_weight)
    kept = lax.optimization_barrier(first(start_keep, keep_weight))
    partial = kept + swap(given, "term", PAIR)
    current = jnp.concatenate(sum_groups(partial), axis=0) * (-TAYLOR_STEP)
    total = current

    gram_left = contract("ij,kj->ik", prefix, prefix)
    gram_right = contract("ji,jk->ik", suffix, suffix)

    turned = product(product(gram_left, current), gram_right)
    partial = apply_terms(turned, left_edge, right_edge, keep_weight)
    partial = partial + apply_terms(turned, other_left, other_right, others)
    current = jnp.concatenate(sum_groups(partial), axis=0) * (-TAYLOR_STEP / 2)
    total = total + current

    weights = jnp.concatenate([keep_weight, others])
    lefts = jnp.concatenate([left_edge, other_left], axis=0)
    rights = jnp.concatenate([right_edge, other_right], axis=0)
    lefts = contract("tij,jk->tik", lefts, gram_left) * weights[:, None, None]
    rights = contract("ij,tjk->tik", gram_right, rights)

    for order in range(3, ORDER):
        partial = apply_terms(current, lefts, rights)
        current = jnp.concatenate(sum_groups(partial), axis=0)
        current = current * (-TAYLOR_STEP / order)
        total = total + current

    partial = apply_terms(current, lefts, rights) * (-TAYLOR_STEP / ORDER)
    partial = contract("ij,kj->ik", contract("ji,jk->ik", prefix, partial), suffix)
    so_far = start_keep + contract("ij,kj->ik", contract("ji,jk->ik", prefix, total), suffix)
    ends = sum_groups(partial)
    ours, theirs = [], []
    for i, end in enumerate(ends):
        rows = end.shape[0]
        end = lax.optimization_barrier(so_far[i * rows : (i + 1) * rows]) + end
        ours.append(end)
        theirs.append(swap(end, "term", PAIR))
    ours, theirs = jnp.concatenate(ours, axis=0), jnp.concatenate(theirs, axis=0)
    evolved = jnp.stack(
        [jnp.where(mine == 0, ours, theirs), jnp.where(mine == 0, theirs, ours)]
    )
    return evolved[None]


def solution(mesh):
    in_specs = (
        P("sec", None, None, None),
        P("sec", None, None),
        P("sec"),
        P("term", None, None),
        P("term", None, None),
        P(),
        P("term"),
        P(),
    )
    out_specs = P("sec", None, None, None)
    return jax.shard_map(
        on_device, mesh=mesh, in_specs=in_specs, out_specs=out_specs, check_vma=False
    )
```
